32 devices in a mesh: ta: 8 (over z, x), sa: 4 (over y, core).
Axes of the slice: x: 2, y: 2, z: 4, core: 2. Of those that a mesh axis runs over, the one named last changes fastest.
Arguments:
- temporal_links: float32 [18, 32, 8, 384], P(None, 'ta', 'sa'), may hold values from -1 to 1, as said below
- spatial_links: float32 [3, 18, 32, 8, 384], P(None, None, 'ta', 'sa'), may hold values from -1 to 1, as said below
- rotations: float32 [3, 3, 4, 32, 8, 384], P(None, None, None, 'ta', 'sa'), may hold values from -1 to 1, as said below
Outputs:
- transfer: float32 [2, 9, 9, 8, 8, 384], P(None, None, None, 'ta', 'sa')
- log_scale: float32 [8, 8, 384], P('ta', 'sa')
The draws below stay inside these ranges and needn't reach their ends.
Inputs may be any that keep to these rules, and one draw needn't show every extreme that they name: `temporal_links`: every link's 3x3 complex matrix is special unitary. `spatial_links`: every link's 3x3 complex matrix is special unitary. `rotations`: the four entries along the third dimension form a unit quaternion.
All inputs are finite; a program needn't handle non-finite values.
Results may differ from the reference program's by a relative error of at most 0.0003.
Values sent between devices are 32-bit elements; how exact they have to be, the bound alone decides.
No kernel may reach another device: no remote copies, remote signals or barrier semaphores. Data moves between devices by JAX's collectives and lax.ppermute only.
A program may use at most 128 MiB of HBM per device.

```python
import math
import jax
import jax.numpy as jnp
from jax import lax

SLAB = 4
SWEEPS = 3
DIST = 4
LZ = 16
NT = 32
LX = 8
LYZ = 384


def unit_quaternion(key, shape, spread):
    key_polar, key_tilt, key_turn = jax.random.split(key, 3)
    polar = jax.random.uniform(key_polar, shape, jnp.float32, 0.0, spread)
    tilt = jax.random.uniform(key_tilt, shape, jnp.float32, 0.0, math.pi)
    turn = jax.random.uniform(key_turn, shape, jnp.float32, -math.pi, math.pi)
    sine = jnp.sin(polar)
    return [jnp.cos(polar), sine * jnp.cos(tilt), sine * jnp.sin(tilt) * jnp.cos(turn), sine * jnp.sin(tilt) * jnp.sin(turn)]


def block_matrix(quaternion, upper_row, lower_row, shape):
    zeros = jnp.zeros(shape, jnp.float32)
    ones = jnp.ones(shape, jnp.float32)
    matrix = [[(ones if row_idx == col_idx else zeros, zeros) for col_idx in range(3)] for row_idx in range(3)]
    matrix[upper_row][upper_row] = (quaternion[0], quaternion[3])
    matrix[upper_row][lower_row] = (quaternion[2], quaternion[1])
    matrix[lower_row][upper_row] = (-quaternion[2], quaternion[1])
    matrix[lower_row][lower_row] = (quaternion[0], -quaternion[3])
    return matrix


def list_product(left_rows, right_rows):
    result = []
    for row_idx in range(3):
        row_list = []
        for col_idx in range(3):
            real_sum = 0.0
            imag_sum = 0.0
            for inner_idx in range(3):
                left_entry = left_rows[row_idx][inner_idx]
                right_entry = right_rows[inner_idx][col_idx]
                real_sum = real_sum + left_entry[0] * right_entry[0] - left_entry[1] * right_entry[1]
                imag_sum = imag_sum + left_entry[0] * right_entry[1] + left_entry[1] * right_entry[0]
            row_list.append((real_sum, imag_sum))
        result.append(row_list)
    return result


def special_unitary(key, shape, spread):
    keys = jax.random.split(key, 5)
    result = block_matrix(unit_quaternion(keys[0], shape, spread), 0, 1, shape)
    result = list_product(result, block_matrix(unit_quaternion(keys[1], shape, spread), 1, 2, shape))
    result = list_product(result, block_matrix(unit_quaternion(keys[2], shape, spread), 0, 1, shape))
    alpha = jax.random.uniform(keys[3], shape, jnp.float32, -spread, spread)
    beta = jax.random.uniform(keys[4], shape, jnp.float32, -spread, spread)
    zeros = jnp.zeros(shape, jnp.float32)
    phases = [[(zeros, zeros) for col_idx in range(3)] for row_idx in range(3)]
    phases[0][0] = (jnp.cos(alpha), jnp.sin(alpha))
    phases[1][1] = (jnp.cos(beta), jnp.sin(beta))
    phases[2][2] = (jnp.cos(alpha + beta), -jnp.sin(alpha + beta))
    result = list_product(result, phases)
    reals = [result[row_idx][col_idx][0] for row_idx in range(3) for col_idx in range(3)]
    imags = [result[row_idx][col_idx][1] for row_idx in range(3) for col_idx in range(3)]
    return reals + imags


def draw_temporal_links(key, part):
    spread = math.pi
    entries = special_unitary(jax.random.fold_in(key, 11), (NT, LX, LYZ), spread)
    return jnp.stack(entries, axis=0)


def draw_spatial_links(key, part):
    spread = math.pi
    entries = special_unitary(jax.random.fold_in(key, 23), (3, NT, LX, LYZ), spread)
    return jnp.stack(entries, axis=1)


def draw_rotations(key, part):
    spread = math.pi
    entries = unit_quaternion(jax.random.fold_in(key, 37), (SWEEPS, 3, NT, LX, LYZ), spread)
    return jnp.stack(entries, axis=2)


def setup_inputs(seed: int = 0) -> dict:
    key_of = jax.random.split(jax.random.key(seed), 4)
    temporal_links = draw_temporal_links(jax.random.fold_in(key_of[3], 71), 0)
    spatial_links = draw_spatial_links(jax.random.fold_in(key_of[3], 71), 0)
    rotations = draw_rotations(jax.random.fold_in(key_of[3], 71), 0)
    return {"temporal_links": temporal_links, "spatial_links": spatial_links, "rotations": rotations}


def tree_apply(function, pair):
    return (function(pair[0]), function(pair[1]))

def as_pair(links):
    shaped = links.reshape((2, 3, 3) + links.shape[1:])
    return (shaped[0], shaped[1])

def as_flat(pair):
    return jnp.stack(pair).reshape((18,) + pair[0].shape[2:])

def complex_mul(left_pair, right_pair):
    out_real = 0.0
    out_imag = 0.0
    for inner_idx in range(left_pair[0].shape[1]):
        row_real = left_pair[0][:, inner_idx:inner_idx + 1]
        row_imag = left_pair[1][:, inner_idx:inner_idx + 1]
        col_real = right_pair[0][inner_idx:inner_idx + 1]
        col_imag = right_pair[1][inner_idx:inner_idx + 1]
        out_real = out_real + row_real * col_real - row_imag * col_imag
        out_imag = out_imag + row_real * col_imag + row_imag * col_real
    return (out_real, out_imag)

def triple(first_pair, middle_pair, last_pair):
    return complex_mul(complex_mul(first_pair, middle_pair), last_pair)

def dagger(matrix):
    return (jnp.swapaxes(matrix[0], 0, 1), -jnp.swapaxes(matrix[1], 0, 1))

def add_pair(left_pair, right_pair):
    return (left_pair[0] + right_pair[0], left_pair[1] + right_pair[1])

def scalar_mul(left_pair, right_pair):
    return (left_pair[0] * right_pair[0] - left_pair[1] * right_pair[1], left_pair[0] * right_pair[1] + left_pair[1] * right_pair[0])

def shift_rows(values, offset):
    return jnp.roll(values, -offset * LZ, axis=-1)

def shift_depth(values, offset):
    position = jnp.arange(values.shape[-1]) % LZ
    if offset > 0:
        return jnp.where(position + offset >= LZ, jnp.roll(values, LZ - offset, axis=-1), jnp.roll(values, -offset, axis=-1))
    return jnp.where(position + offset < 0, jnp.roll(values, -LZ - offset, axis=-1), jnp.roll(values, -offset, axis=-1))

def later_slices(member):
    return member[:, :, 1:]

def now_slices(member):
    return member[:, :, :-1]

def rotate_rows(matrix, upper_row, lower_row, blocks):
    rows_real = [matrix[0][row_idx] for row_idx in range(3)]
    rows_imag = [matrix[1][row_idx] for row_idx in range(3)]
    upper_pair = (rows_real[upper_row], rows_imag[upper_row])
    lower_pair = (rows_real[lower_row], rows_imag[lower_row])
    new_upper = add_pair(scalar_mul(blocks[0], upper_pair), scalar_mul(blocks[1], lower_pair))
    new_lower = add_pair(scalar_mul(blocks[2], upper_pair), scalar_mul(blocks[3], lower_pair))
    rows_real[upper_row] = new_upper[0]
    rows_imag[upper_row] = new_upper[1]
    rows_real[lower_row] = new_lower[0]
    rows_imag[lower_row] = new_lower[1]
    return (jnp.stack(rows_real), jnp.stack(rows_imag))

def relax(temporal, center, left_x, rotation, parity, first_col):
    col_count = rotation.shape[3]
    own_links = tree_apply(lambda member: member[..., 1:col_count + 1, :], temporal)
    ahead_links = tree_apply(lambda member: member[..., 2:col_count + 2, :], temporal)
    behind = tree_apply(lambda member: member[..., 0:col_count, :], temporal)
    staple = add_pair(triple(tree_apply(later_slices, center[0]), dagger(ahead_links), dagger(tree_apply(now_slices, center[0]))), triple(dagger(tree_apply(later_slices, left_x)), dagger(behind), tree_apply(now_slices, left_x)))
    for direction, shifter in ((1, shift_rows), (2, shift_depth)):
        side_link = center[direction]
        back_link = tree_apply(lambda member: shifter(member, -1), side_link)
        forward_time = tree_apply(lambda member: shifter(member, 1), own_links)
        backward_time = tree_apply(lambda member: shifter(member, -1), own_links)
        staple = add_pair(staple, add_pair(triple(tree_apply(later_slices, side_link), dagger(forward_time), dagger(tree_apply(now_slices, side_link))), triple(dagger(tree_apply(later_slices, back_link)), dagger(backward_time), tree_apply(now_slices, back_link))))
    product = complex_mul(own_links, staple)
    updated = own_links
    for subgroup, (upper_row, lower_row) in enumerate(((0, 1), (1, 2), (0, 2))):
        prod_real, prod_imag = product
        stat_zero = 0.5 * (prod_real[upper_row, upper_row] + prod_real[lower_row, lower_row])
        stat_one = 0.5 * (prod_imag[upper_row, lower_row] + prod_imag[lower_row, upper_row])
        stat_two = 0.5 * (prod_real[upper_row, lower_row] - prod_real[lower_row, upper_row])
        stat_three = 0.5 * (prod_imag[upper_row, upper_row] - prod_imag[lower_row, lower_row])
        vec_sq = stat_one * stat_one + stat_two * stat_two + stat_three * stat_three
        norm_sq = jnp.maximum(stat_zero * stat_zero + vec_sq, 0.5)
        refl_zero = (stat_zero * stat_zero - vec_sq) / norm_sq
        refl_one = -2.0 * stat_zero * stat_one / norm_sq
        refl_two = -2.0 * stat_zero * stat_two / norm_sq
        refl_three = -2.0 * stat_zero * stat_three / norm_sq
        turn_zero = rotation[subgroup, 0]
        turn_one = rotation[subgroup, 1]
        turn_two = rotation[subgroup, 2]
        turn_three = rotation[subgroup, 3]
        new_zero = turn_zero * refl_zero - (turn_one * refl_one + turn_two * refl_two + turn_three * refl_three)
        new_one = turn_zero * refl_one + refl_zero * turn_one - (turn_two * refl_three - turn_three * refl_two)
        new_two = turn_zero * refl_two + refl_zero * turn_two - (turn_three * refl_one - turn_one * refl_three)
        new_three = turn_zero * refl_three + refl_zero * turn_three - (turn_one * refl_two - turn_two * refl_one)
        blocks = ((new_zero, new_three), (new_two, new_one), (-new_two, new_one), (new_zero, -new_three))
        updated = rotate_rows(updated, upper_row, lower_row, blocks)
        product = rotate_rows(product, upper_row, lower_row, blocks)
    col_pos = first_col + jnp.arange(col_count)
    flat_pos = jnp.arange(own_links[0].shape[-1])
    parity_mask = (col_pos[:, None] + flat_pos[None, :] // LZ + flat_pos[None, :] % LZ) % 2 == parity
    return (jnp.where(parity_mask, updated[0], own_links[0]), jnp.where(parity_mask, updated[1], own_links[1]))

def slab_operator(links):
    product = tree_apply(lambda member: member[:, :, 0], links)
    for time_idx in range(1, links[0].shape[2]):
        product = complex_mul(product, tree_apply(lambda member: member[:, :, time_idx], links))
    partner = tree_apply(lambda member: shift_depth(member, DIST), product)
    col_count = product[0].shape[2]
    site_count = product[0].shape[3]
    left_real = product[0][:, None, :, None]
    left_imag = product[1][:, None, :, None]
    right_real = partner[0][None, :, None, :]
    right_imag = partner[1][None, :, None, :]
    real_part = (left_real * right_real + left_imag * right_imag).reshape(9, 9, col_count, site_count)
    imag_part = (left_imag * right_real - left_real * right_imag).reshape(9, 9, col_count, site_count)
    return (real_part, imag_part)

def normalize(real_part, imag_part):
    mean_sq = (lax.optimization_barrier(jnp.sum(real_part * real_part, axis=(0, 1))) + lax.optimization_barrier(jnp.sum(imag_part * imag_part, axis=(0, 1)))) / 162.0
    rms_scale = jnp.sqrt(mean_sq + 1e-06)
    return (real_part / rms_scale, imag_part / rms_scale, jnp.log(rms_scale))

def chain_combine(earlier, later):
    prod_real, prod_imag = complex_mul((earlier[0], earlier[1]), (later[0], later[1]))
    real_part, imag_part, extra_log = normalize(prod_real, prod_imag)
    return (real_part, imag_part, earlier[2] + later[2] + extra_log)

def slab_pass(inputs):
    temporal, spatial_ext, rotation = inputs
    center = [as_pair(spatial_ext[dir_idx]) for dir_idx in range(3)]
    left_x = as_pair(jnp.roll(spatial_ext[0], 1, axis=2))
    current = temporal
    for sweep_idx in range(SWEEPS):
        for parity in (0, 1):
            padded = jnp.concatenate([current[:, :, -1:], current, current[:, :, :1]], axis=2)
            current = as_flat(relax(as_pair(padded), center, left_x, rotation[sweep_idx], parity, 0))
        real_part, imag_part = slab_operator(as_pair(current))
        if sweep_idx == 0:
            total_real, total_imag = (real_part, imag_part)
        else:
            total_real = total_real + real_part
            total_imag = total_imag + imag_part
    return normalize(total_real * (1.0 / SWEEPS), total_imag * (1.0 / SWEEPS))

def reference(temporal_links, spatial_links, rotations):
    slab_count = NT // SLAB
    temporal_slabs = jnp.moveaxis(temporal_links.reshape(18, slab_count, SLAB, LX, LYZ), 1, 0)
    spatial_slabs = spatial_links.reshape(3, 18, slab_count, SLAB, LX, LYZ)
    next_first = jnp.roll(spatial_slabs[:, :, :, 0:1], -1, axis=2)
    spatial_ext = jnp.moveaxis(jnp.concatenate([spatial_slabs, next_first], axis=3), 2, 0)
    rotation_slabs = jnp.moveaxis(rotations.reshape(SWEEPS, 3, 4, slab_count, SLAB, LX, LYZ), 3, 0)
    averaged = lax.map(slab_pass, (temporal_slabs, spatial_ext, rotation_slabs))
    eye_real = jnp.broadcast_to(jnp.eye(9, dtype=temporal_links.dtype)[:, :, None, None], (9, 9, LX, LYZ))
    initial = (eye_real, jnp.zeros_like(eye_real), jnp.zeros((LX, LYZ), temporal_links.dtype))

    def advance(carry, piece):
        combined = chain_combine(carry, piece)
        return (combined, combined)
    final_state, chain_all = lax.scan(advance, initial, averaged)
    transfer = jnp.stack([jnp.moveaxis(chain_all[0], 0, 2), jnp.moveaxis(chain_all[1], 0, 2)])
    return (transfer, chain_all[2])
```

```python
import functools

import jax
import jax.numpy as jnp
from jax import lax
from jax.experimental import pallas as pl
from jax.experimental.pallas import tpu as pltpu
from jax.sharding import PartitionSpec as P

DIST = 4
LZ = 16
LANES = 128
EPS = 1e-06
F32 = jnp.float32
SPEC = pl.BlockSpec(memory_space=pltpu.VMEM)
PAIRS = ((0, 1), (1, 2), (0, 2))


class Dims:
    def __init__(self, temporal, rotations, ta, sa):
        self.slices, self.cols, self.width = temporal.shape[1:]
        self.sweeps = rotations.shape[0]
        self.ta, self.sa = ta, sa
        self.blocks = self.width // LANES
        self.pairs = self.slices // 2
        self.group = self.pairs * self.cols
        self.rows = self.blocks * self.group
        self.edge = self.blocks * self.pairs
        self.flat = self.blocks * self.cols
        assert self.width % LANES == 0 and self.slices % 2 == 0 and sa % 2 == 0
        assert LANES % ta == 0 and LANES % LZ == 0
        self.lane_share = LANES // ta
        self.whole_z = self.lane_share % LZ == 0
        self.l_comps = 18 if self.whole_z else 36
        self.l_blocks = -(-self.l_comps * self.flat // ta)
        self.t_blocks = -(-(162 + 1) * self.flat // ta)


def iota(shape, dim):
    return lax.broadcasted_iota(jnp.int32, shape, dim)


def parity_of(dims):
    row, lane = iota((dims.rows, LANES), 0), iota((dims.rows, LANES), 1)
    y = row // dims.group * (LANES // LZ) + lane // LZ
    first = lax.axis_index("sa") * dims.cols if dims.cols % 2 else 0
    return (first + row % dims.cols + y + lane % LZ) % 2


def y_move(dims, value, step):
    lane = iota(value.shape, 1)
    size = dims.group
    if step > 0:
        turned = pltpu.roll(value, LANES - LZ, 1)
        other = jnp.concatenate([turned[size:], turned[:size]], axis=0)
        return jnp.where(lane < LANES - LZ, turned, other)
    turned = pltpu.roll(value, LZ, 1)
    other = jnp.concatenate([turned[-size:], turned[:-size]], axis=0)
    return jnp.where(lane >= LZ, turned, other)


def z_move(value, step):
    z = iota(value.shape, 1) % LZ
    if step > 0:
        return jnp.where(
            z + step >= LZ, pltpu.roll(value, LZ - step, 1), pltpu.roll(value, LANES - step, 1)
        )
    return jnp.where(
        z + step < 0, pltpu.roll(value, LANES - LZ - step, 1), pltpu.roll(value, -step, 1)
    )


def product(left, right, left_dagger=False, right_dagger=False):
    out = []
    for i in range(3):
        for j in range(3):
            real = imag = None
            for k in range(3):
                a, b = left[3 * k + i] if left_dagger else left[3 * i + k]
                c, d = right[3 * j + k] if right_dagger else right[3 * k + j]
                if left_dagger == right_dagger:
                    more_real, more_imag = a * c - b * d, a * d + b * c
                    if left_dagger:
                        more_imag = -more_imag
                elif left_dagger:
                    more_real, more_imag = a * c + b * d, a * d - b * c
                else:
                    more_real, more_imag = a * c + b * d, b * c - a * d
                real = more_real if real is None else real + more_real
                imag = more_imag if imag is None else imag + more_imag
            out.append((real, imag))
    return out


def matrix(ref, rows, *index):
    return [(ref[(*index, c, rows)], ref[(*index, 9 + c, rows)]) for c in range(9)]


def put(ref, rows, entries, *index):
    for c in range(9):
        ref[(*index, c, rows)] = entries[c][0]
        ref[(*index, 9 + c, rows)] = entries[c][1]


def added(left, right):
    return [(a + c, b + d) for (a, b), (c, d) in zip(left, right)]


def chunks(rows):
    return [slice(start, min(start + 8, rows)) for start in range(0, rows, 8)]


def call(body, operands, shapes, scratch=(), flops=0):
    operands = [pltpu.with_memory_space_constraint(x, pltpu.VMEM) for x in operands]
    return pl.pallas_call(
        body,
        out_shape=[pltpu.VMEM(shape, F32) for shape in shapes],
        in_specs=[SPEC] * len(operands),
        out_specs=[SPEC] * len(shapes),
        scratch_shapes=[pltpu.VMEM(shape, F32) for shape in scratch],
        compiler_params=pltpu.CompilerParams(vmem_limit_bytes=24 << 20),
        cost_estimate=pl.CostEstimate(flops=flops, bytes_accessed=flops // 4, transcendentals=0),
    )(*operands)


def pack_body(dims, t_ref, s_ref, r_ref, q_ref, now_ref, odd_ref, next_ref, rot_ref, even, odd):
    parity = parity_of(dims)

    def gather(source, slot):
        for block in range(dims.blocks):
            lanes = slice(block * LANES, (block + 1) * LANES)
            for pair in range(dims.pairs):
                start = block * dims.group + pair * dims.cols
                rows = slice(start, start + dims.cols)
                even[slot, rows, :] = source(2 * pair, lanes)
                odd[slot, rows, :] = source(2 * pair + 1, lanes)

    def temporal(c, _):
        gather(lambda t, lanes: t_ref[c, t, :, lanes], 0)
        moved = y_move(dims, odd[0], -1)
        for q in range(2):
            q_ref[q, c] = jnp.where(parity == q, even[0], moved)
        return 0

    lax.fori_loop(0, 18, temporal, 0, unroll=2)

    def spatial(c, _):
        for k in range(3):
            gather(lambda t, lanes: s_ref[k, c, t, :, lanes], k)
            moved = y_move(dims, odd[k], -1)
            for q in range(2):
                now_ref[q, k, c] = jnp.where(parity == q, even[k], moved)
            odd_ref[k, c] = odd[k]
            for block in range(dims.blocks):
                start = block * dims.group
                next_ref[k, c, start : start + dims.group - dims.cols] = even[
                    k, start + dims.cols : start + dims.group
                ]
        return 0

    lax.fori_loop(0, 18, spatial, 0)

    def turns(sweep, _):
        for g in range(3):
            for c in range(4):
                slot = g * 4 + c
                gather(lambda t, lanes: r_ref[sweep, g, c, t, :, lanes], slot)
                moved = y_move(dims, odd[slot], -1)
                for q in range(2):
                    rot_ref[sweep, q, g, c] = jnp.where(parity == q, even[slot], moved)
        return 0

    lax.fori_loop(0, dims.sweeps, turns, 0)


def pack(dims, temporal, spatial, rotations):
    shape = (dims.rows, LANES)
    shapes = [
        (2, 18, *shape),
        (2, 3, 18, *shape),
        (3, 18, *shape),
        (3, 18, *shape),
        (dims.sweeps, 2, 3, 4, *shape),
    ]
    return pl.pallas_call(
        functools.partial(pack_body, dims),
        out_shape=[pltpu.VMEM(s, F32) for s in shapes],
        in_specs=[SPEC] * 3,
        out_specs=[SPEC] * 5,
        scratch_shapes=[pltpu.VMEM((12, *shape), F32)] * 2,
        compiler_params=pltpu.CompilerParams(vmem_limit_bytes=24 << 20),
        cost_estimate=pl.CostEstimate(flops=4000000, bytes_accessed=4000000, transcendentals=0),
    )(temporal, spatial, rotations)


def emit(dims, links, back, msg_own, msg_other):
    even = lax.axis_index("sa") % 2 == 0

    def fill(right, left):
        for c in range(18):
            rows = slice(c * dims.edge, (c + 1) * dims.edge)
            right[rows, :] = back[c, pl.ds(dims.cols - 1, dims.edge, stride=dims.cols), :]
            left[rows, :] = links[c, pl.ds(0, dims.edge, stride=dims.cols), :]

    pl.when(even)(lambda: fill(msg_own, msg_other))
    pl.when(jnp.logical_not(even))(lambda: fill(msg_other, msg_own))


def absorb(dims, got_own, got_other, ahead, behind):
    even = lax.axis_index("sa") % 2 == 0

    def fill(from_right, from_left):
        for c in range(18):
            rows = slice(c * dims.edge, (c + 1) * dims.edge)
            ahead[c, pl.ds(dims.cols - 1, dims.edge, stride=dims.cols), :] = from_right[rows, :]
            behind[c, pl.ds(0, dims.edge, stride=dims.cols), :] = from_left[rows, :]

    pl.when(even)(lambda: fill(got_own, got_other))
    pl.when(jnp.logical_not(even))(lambda: fill(got_other, got_own))


def backward(dims, links, now, later, out, parity, direction):
    for rows in chunks(dims.rows):
        inner = product(
            matrix(links, rows), matrix(now, rows, parity, direction), left_dagger=True
        )
        put(
            out,
            rows,
            product(matrix(later, rows, parity, direction), inner, left_dagger=True),
        )


def first_body(dims, q, now, odd, nxt, nf, later, back, msg_own, msg_other, even):
    parity = parity_of(dims)
    last = dims.pairs - 1

    def one(c, _):
        for k in range(3):
            for block in range(dims.blocks):
                start = block * dims.group
                even[k, start : start + last * dims.cols] = nxt[
                    k, c, start : start + last * dims.cols
                ]
                even[k, start + last * dims.cols : start + dims.group] = nf[
                    k, c, :, block * LANES : (block + 1) * LANES
                ]
            moved = y_move(dims, even[k], -1)
            value = odd[k, c]
            for p in range(2):
                later[p, k, c] = jnp.where(parity == p, value, moved)
        return 0

    lax.fori_loop(0, 18, one, 0, unroll=2)
    backward(dims, q.at[1], now, later, back, 1, 0)
    emit(dims, q.at[1], back, msg_own, msg_other)


def inner_body(dims, p, other, now, later, out, moved, back):
    for direction, move in ((1, functools.partial(y_move, dims)), (2, z_move)):
        for c in range(18):
            moved[c] = move(other[c], 1)
        backward(dims, other, now, later, back, 1 - p, direction)
        for c in range(18):
            shifted = move(back[c], -1)
            out[c] = shifted if direction == 1 else out[c] + shifted
        for rows in chunks(dims.rows):
            half = product(matrix(now, rows, p, direction), matrix(moved, rows))
            term = product(matrix(later, rows, p, direction), half, right_dagger=True)
            put(out, rows, added(matrix(out, rows), term))


def rotate(entries, upper, lower, turn):
    a0, a1, a2, a3 = turn
    out = list(entries)
    for col in range(3):
        ur, ui = entries[3 * upper + col]
        lr, li = entries[3 * lower + col]
        out[3 * upper + col] = (
            (a0 * ur - a3 * ui) + (a2 * lr - a1 * li),
            (a0 * ui + a3 * ur) + (a2 * li + a1 * lr),
        )
        out[3 * lower + col] = (
            (a0 * lr + a3 * li) - (a2 * ur + a1 * ui),
            (a0 * li - a3 * lr) + (a1 * ur - a2 * ui),
        )
    return out


def update(links, staple, turns):
    field = product(links, staple)
    for g, (i, j) in enumerate(PAIRS):
        w0 = 0.5 * (field[4 * i][0] + field[4 * j][0])
        w1 = 0.5 * (field[3 * i + j][1] + field[3 * j + i][1])
        w2 = 0.5 * (field[3 * i + j][0] - field[3 * j + i][0])
        w3 = 0.5 * (field[4 * i][1] - field[4 * j][1])
        v = w1 * w1 + w2 * w2 + w3 * w3
        square = w0 * w0
        inverse = 1.0 / jnp.maximum(square + v, 0.5)
        r0 = (square - v) * inverse
        twice = (-2.0 * w0) * inverse
        r1, r2, r3 = twice * w1, twice * w2, twice * w3
        x0, x1, x2, x3 = turns[g]
        turn = (
            x0 * r0 - (x1 * r1 + x2 * r2 + x3 * r3),
            x0 * r1 + r0 * x1 - (x2 * r3 - x3 * r2),
            x0 * r2 + r0 * x2 - (x3 * r1 - x1 * r3),
            x0 * r3 + r0 * x3 - (x1 * r2 - x2 * r1),
        )
        links = rotate(links, i, j, turn)
        if g < 2:
            field = rotate(field, i, j, turn)
    return links


def outer_body(dims, p, sweep, last, *refs):
    own, other, now, later, rot, partial, back, got_own, got_other = refs[:9]
    new, ahead, behind = refs[9], refs[-2], refs[-1]
    for c in range(18):
        for col in range(dims.cols - 1):
            here = pl.ds(col, dims.edge, stride=dims.cols)
            there = pl.ds(col + 1, dims.edge, stride=dims.cols)
            ahead[c, here, :] = other[c, there, :]
            behind[c, there, :] = back[c, here, :]
    absorb(dims, got_own, got_other, ahead, behind)
    for rows in chunks(dims.rows):
        half = product(matrix(now, rows, p, 0), matrix(ahead, rows))
        term = product(matrix(later, rows, p, 0), half, right_dagger=True)
        staple = added(added(matrix(partial, rows), matrix(behind, rows)), term)
        turns = [[rot[sweep, p, g, c, rows] for c in range(4)] for g in range(3)]
        put(new, rows, update(matrix(own, rows), staple, turns))
    if not last:
        new_back, msg_own, msg_other = refs[10:13]
        backward(dims, new, now, later, new_back, p, 0)
        emit(dims, new, new_back, msg_own, msg_other)


def loop_body(dims, q0, q1, out, pair, parts):
    parity = parity_of(dims)
    even, odd = [], []
    for c in range(18):
        a, b = q0[c], q1[c]
        pair[0, c] = jnp.where(parity == 0, a, b)
        pair[1, c] = y_move(dims, jnp.where(parity == 0, b, a), 1)
    for rows in chunks(dims.rows):
        put(
            pair,
            rows,
            product(matrix(pair, rows, 0), matrix(pair, rows, 1)),
            2,
        )
    for c in range(18):
        for k in range(dims.pairs):
            for col in range(dims.cols):
                parts[k, c, pl.ds(col, dims.blocks, stride=dims.cols), :] = pair[
                    2, c, pl.ds(k * dims.cols + col, dims.blocks, stride=dims.group), :
                ]
    every = slice(0, dims.flat)
    total = matrix(parts, every, 0)
    for k in range(1, dims.pairs):
        total = product(total, matrix(parts, every, k))
    for c in range(9):
        for half in range(2):
            start = (9 * half + c) * dims.flat
            out[start : start + dims.flat, :] = total[c][half]
            if not dims.whole_z:
                start += 18 * dims.flat
                out[start : start + dims.flat, :] = z_move(total[c][half], DIST)
    used = dims.l_comps * dims.flat
    if used < out.shape[0]:
        out[used:, :] = jnp.zeros((out.shape[0] - used, LANES), F32)


def exchange_blocks(dims, value):
    n, width = dims.ta, dims.lane_share
    row = iota((n, LANES), 0)
    group = iota((n, LANES), 1) // width
    step = n // 2
    while step:
        row_bit, group_bit = (row // step) % 2, (group // step) % 2
        up = pltpu.roll(pltpu.roll(value, n - step, 0), width * step, 1)
        down = up
        if 2 * step != n:
            down = pltpu.roll(pltpu.roll(value, step, 0), LANES - width * step, 1)
        value = jnp.where(row_bit == group_bit, value, jnp.where(row_bit == 0, up, down))
        step //= 2
    return value


def spread_body(dims, *refs):
    sources, outs = refs[: dims.sweeps], refs[dims.sweeps :]
    place = lax.axis_index("ta")
    n = dims.ta
    for sweep, source in enumerate(sources):
        for k in range(dims.l_blocks):
            value = exchange_blocks(dims, source[k * n : (k + 1) * n, :])
            value = pltpu.roll(value, (n - place) % n, 0)
            at = sweep * dims.l_blocks + k
            for d in range(n):
                outs[d][at : at + 1, :] = value[d : d + 1, :]


def log_add(left, right):
    top = jnp.maximum(left, right)
    low = jnp.minimum(left, right)
    return jnp.where(top == low, top + 0.6931471805599453, top + jnp.log(1.0 + jnp.exp(low - top)))


def collect(dims, sources, stack, blocks):
    n = dims.ta
    place = lax.axis_index("ta")
    for e in range(n):
        stack[e * blocks : (e + 1) * blocks, :] = sources[(n - e) % n][...]
    for k in range(blocks):
        value = stack[pl.ds(k, n, stride=blocks), :]
        yield k, exchange_blocks(dims, pltpu.roll(value, place, 0))


def chain_body(dims, *refs):
    n = dims.ta
    sources, outs = refs[:n], refs[n : 2 * n]
    stack, loops, mats, temp, flat = refs[2 * n :]
    place = lax.axis_index("ta")
    rows, width = dims.flat, dims.lane_share
    shape = (rows, LANES)
    for k, value in collect(dims, sources, stack, dims.sweeps * dims.l_blocks):
        loops[k * n : (k + 1) * n, :] = value
    size = dims.l_blocks * n

    def entry(sweep, c):
        start = sweep * size + c * rows
        return loops[start : start + rows, :]

    shifted = [
        [
            z_move(entry(s, c), DIST) if dims.whole_z else entry(s, 18 + c)
            for c in range(18)
        ]
        for s in range(dims.sweeps)
    ]
    for s in range(dims.sweeps):
        for c in range(18):
            temp[s * 18 + c] = shifted[s][c]
    total = jnp.zeros(shape, F32)
    for a in range(3):
        for e in range(3):
            left = [(entry(s, 3 * a + e), entry(s, 9 + 3 * a + e)) for s in range(dims.sweeps)]
            for c in range(3):
                for d in range(3):
                    real = imag = None
                    for s in range(dims.sweeps):
                        lr, li = left[s]
                        pr, pi = temp[s * 18 + 3 * c + d], temp[s * 18 + 9 + 3 * c + d]
                        more_real, more_imag = lr * pr + li * pi, li * pr - lr * pi
                        real = more_real if real is None else real + more_real
                        imag = more_imag if imag is None else imag + more_imag
                    real, imag = real * (1.0 / dims.sweeps), imag * (1.0 / dims.sweeps)
                    at = 9 * (3 * a + c) + 3 * e + d
                    mats[0, at] = real
                    mats[0, 81 + at] = imag
                    total = total + (real * real + imag * imag)
    group = iota(shape, 1) // width
    norm = 0.5 * jnp.log(total / 162.0 + EPS)
    scale = -norm
    step, now = 1, 0
    while step < n:
        def one_row(i, total):
            left = [
                (
                    pltpu.roll(mats[now, 9 * i + k], width * step, 1),
                    pltpu.roll(mats[now, 81 + 9 * i + k], width * step, 1),
                )
                for k in range(9)
            ]
            for j in range(9):
                real = imag = None
                for k in range(9):
                    a, b = left[k]
                    c, d = mats[now, 9 * k + j], mats[now, 81 + 9 * k + j]
                    more_real, more_imag = a * c - b * d, a * d + b * c
                    real = more_real if real is None else real + more_real
                    imag = more_imag if imag is None else imag + more_imag
                mats[1 - now, 9 * i + j] = real
                mats[1 - now, 81 + 9 * i + j] = imag
                total = total + (real * real + imag * imag)
            return total

        total = lax.fori_loop(0, 9, one_row, jnp.zeros(shape, F32))
        active = group >= step
        square = total / 162.0 + EPS
        factor = 1.0 / jnp.sqrt(square)

        def rescale(c, total):
            value = jnp.where(active, mats[1 - now, c] * factor, mats[now, c])
            mats[1 - now, c] = value
            return total + value * value

        total = lax.fori_loop(0, 162, rescale, jnp.zeros(shape, F32), unroll=18)
        scale = jnp.where(
            active, scale + pltpu.roll(scale, width * step, 1) + 0.5 * jnp.log(square), scale
        )
        norm = jnp.where(active, norm + pltpu.roll(norm, width * step, 1), norm)
        now = 1 - now
        step *= 2
    log_eps = jnp.log(jnp.full(shape, EPS, F32))
    size_log = jnp.log(total / 162.0) + 2.0 * scale
    step = 1
    while step < n:
        before = pltpu.roll(size_log, width * step, 1)
        size_log = jnp.where(
            group >= step, log_add(size_log, step * log_eps + before), size_log
        )
        step *= 2
    size_log = 0.5 * log_add(size_log, (group + 1).astype(F32) * log_eps)
    factor = jnp.exp(scale - size_log)
    for c in range(162):
        flat[c * rows : (c + 1) * rows, :] = mats[now, c] * factor
    flat[162 * rows : 163 * rows, :] = norm + size_log
    if flat.shape[0] > 163 * rows:
        flat[163 * rows :, :] = jnp.zeros((flat.shape[0] - 163 * rows, LANES), F32)
    for k in range(dims.t_blocks):
        value = exchange_blocks(dims, flat[k * n : (k + 1) * n, :])
        value = pltpu.roll(value, (n - place) % n, 0)
        for d in range(n):
            outs[d][k : k + 1, :] = value[d : d + 1, :]


def finish_body(dims, *refs):
    n = dims.ta
    sources, (out, log, stack, flat) = refs[:n], refs[n:]
    for k, value in collect(dims, sources, stack, dims.t_blocks):
        flat[k * n : (k + 1) * n, :] = value
    for block in range(dims.blocks):
        lanes = slice(block * LANES, (block + 1) * LANES)
        for c in range(162):
            start = c * dims.flat + block * dims.cols
            out[c, :, lanes] = flat[start : start + dims.cols, :]
        start = 162 * dims.flat + block * dims.cols
        log[:, lanes] = flat[start : start + dims.cols, :]


def per_device(ta, sa, temporal, spatial, rotations):
    dims = Dims(temporal, rotations, ta, sa)
    shape = (dims.rows, LANES)
    nf = lax.ppermute(spatial[:, :, 0], "ta", [((i + 1) % ta, i) for i in range(ta)])
    q, now, odd, nxt, rot = pack(dims, temporal, spatial, rotations)
    message = (18 * dims.edge, LANES)
    later, back, msg_own, msg_other = call(
        functools.partial(first_body, dims),
        [q, now, odd, nxt, nf],
        [(2, 3, 18, *shape), (18, *shape), message, message],
        [(3, *shape)],
        flops=2000000,
    )
    fields = [q[0], q[1]]
    own_pairs = [(i, i ^ 1) for i in range(sa)]
    other_pairs = [(i, (i + 1) % sa if i % 2 else (i - 1) % sa) for i in range(sa)]
    loops = []
    for sweep in range(dims.sweeps):
        for p in range(2):
            last = sweep == dims.sweeps - 1 and p == 1
            got_other = lax.ppermute(msg_other, "sa", other_pairs)
            got_own = lax.ppermute(msg_own, "sa", own_pairs)
            (partial,) = call(
                functools.partial(inner_body, dims, p),
                [fields[1 - p], now, later],
                [(18, *shape)],
                [(18, *shape), (18, *shape)],
                flops=3000000,
            )
            outs = [(18, *shape)] + ([] if last else [(18, *shape), message, message])
            result = call(
                functools.partial(outer_body, dims, p, sweep, last),
                [fields[p], fields[1 - p], now, later, rot, partial, back, got_own, got_other],
                outs,
                [(18, *shape), (18, *shape)],
                flops=3000000,
            )
            fields[p] = result[0]
            if not last:
                back, msg_own, msg_other = result[1:]
        (loop,) = call(
            functools.partial(loop_body, dims),
            fields,
            [(dims.l_blocks * ta, LANES)],
            [(3, 18, *shape), (dims.pairs, 18, dims.flat, LANES)],
            flops=1000000,
        )
        loops.append(loop)
    blocks = dims.sweeps * dims.l_blocks
    shares = call(functools.partial(spread_body, dims), loops, [(blocks, LANES)] * ta)
    around = [[(i, (i + d) % ta) for i in range(ta)] for d in range(ta)]
    shares = [shares[0]] + [lax.ppermute(shares[d], "ta", around[d]) for d in range(1, ta)]
    rows = dims.flat
    shares = call(
        functools.partial(chain_body, dims),
        shares,
        [(dims.t_blocks, LANES)] * ta,
        [
            (ta * blocks, LANES),
            (ta * blocks, LANES),
            (2, 162, rows, LANES),
            (18 * dims.sweeps, rows, LANES),
            (dims.t_blocks * ta, LANES),
        ],
        flops=10000000,
    )
    shares = [shares[0]] + [lax.ppermute(shares[d], "ta", around[d]) for d in range(1, ta)]
    shares = [pltpu.with_memory_space_constraint(x, pltpu.VMEM) for x in shares]
    transfer, log_scale = pl.pallas_call(
        functools.partial(finish_body, dims),
        out_shape=[
            jax.ShapeDtypeStruct((162, dims.cols, dims.width), F32),
            jax.ShapeDtypeStruct((dims.cols, dims.width), F32),
        ],
        in_specs=[SPEC] * ta,
        out_specs=[SPEC] * 2,
        scratch_shapes=[pltpu.VMEM((dims.t_blocks * ta, LANES), F32)] * 2,
        compiler_params=pltpu.CompilerParams(vmem_limit_bytes=16 << 20),
    )(*shares)
    return (
        transfer.reshape(2, 9, 9, 1, dims.cols, dims.width),
        log_scale[None],
    )


def solution(mesh):
    in_specs = (
        P(None, "ta", "sa", None),
        P(None, None, "ta", "sa", None),
        P(None, None, None, "ta", "sa", None),
    )
    out_specs = (P(None, None, None, "ta", "sa", None), P("ta", "sa", None))
    body = functools.partial(per_device, mesh.shape["ta"], mesh.shape["sa"])
    return jax.shard_map(
        body, mesh=mesh, in_specs=in_specs, out_specs=out_specs, check_vma=False
    )
```

```python
import functools


import jax
import jax.numpy as jnp
from jax import lax
from jax.experimental import pallas as pl
from jax.experimental.pallas import tpu as pltpu
from jax.sharding import PartitionSpec as P

DIST = 4
LZ = 16
LANES = 128
EPS = 1e-06
F32 = jnp.float32
SPEC = pl.BlockSpec(memory_space=pltpu.VMEM)
PAIRS = ((0, 1), (1, 2), (0, 2))


class Dims:
    def __init__(self, temporal, rotations, ta, sa):
        self.slices, self.cols, self.width = temporal.shape[1:]
        self.sweeps = rotations.shape[0]
        self.ta, self.sa = ta, sa
        self.blocks = self.width // LANES
        self.pairs = self.slices // 2
        self.group = self.pairs * self.cols
        self.rows = self.blocks * self.group
        self.edge = self.blocks * self.pairs
        self.flat = self.blocks * self.cols
        assert self.width % LANES == 0 and self.slices % 2 == 0 and sa % 2 == 0
        assert LANES % LZ == 0 and ta % 2 == 0
        self.far = ta // 2
        self.loop_rows = 18 * self.flat


def iota(shape, dim):
    return lax.broadcasted_iota(jnp.int32, shape, dim)


def parity_of(dims):
    row, lane = iota((dims.rows, LANES), 0), iota((dims.rows, LANES), 1)
    y = row // dims.group * (LANES // LZ) + lane // LZ
    first = lax.axis_index("sa") * dims.cols if dims.cols % 2 else 0
    return (first + row % dims.cols + y + lane % LZ) % 2


def y_move(dims, value, step):
    lane = iota(value.shape, 1)
    size = dims.group
    if step > 0:
        turned = pltpu.roll(value, LANES - LZ, 1)
        other = jnp.concatenate([turned[size:], turned[:size]], axis=0)
        return jnp.where(lane < LANES - LZ, turned, other)
    turned = pltpu.roll(value, LZ, 1)
    other = jnp.concatenate([turned[-size:], turned[:-size]], axis=0)
    return jnp.where(lane >= LZ, turned, other)


def z_move(value, step):
    z = iota(value.shape, 1) % LZ
    if step > 0:
        return jnp.where(
            z + step >= LZ, pltpu.roll(value, LZ - step, 1), pltpu.roll(value, LANES - step, 1)
        )
    return jnp.where(
        z + step < 0, pltpu.roll(value, LANES - LZ - step, 1), pltpu.roll(value, -step, 1)
    )


def product(left, right, left_dagger=False, right_dagger=False):
    out = []
    for i in range(3):
        for j in range(3):
            real = imag = None
            for k in range(3):
                a, b = left[3 * k + i] if left_dagger else left[3 * i + k]
                c, d = right[3 * j + k] if right_dagger else right[3 * k + j]
                if left_dagger == right_dagger:
                    more_real, more_imag = a * c - b * d, a * d + b * c
                    if left_dagger:
                        more_imag = -more_imag
                elif left_dagger:
                    more_real, more_imag = a * c + b * d, a * d - b * c
                else:
                    more_real, more_imag = a * c + b * d, b * c - a * d
                real = more_real if real is None else real + more_real
                imag = more_imag if imag is None else imag + more_imag
            out.append((real, imag))
    return out


def matrix(ref, rows, *index):
    return [(ref[(*index, c, rows)], ref[(*index, 9 + c, rows)]) for c in range(9)]


def put(ref, rows, entries, *index):
    for c in range(9):
        ref[(*index, c, rows)] = entries[c][0]
        ref[(*index, 9 + c, rows)] = entries[c][1]


def added(left, right):
    return [(a + c, b + d) for (a, b), (c, d) in zip(left, right)]


def chunks(rows):
    return [slice(start, min(start + 8, rows)) for start in range(0, rows, 8)]


def call(body, operands, shapes, scratch=(), flops=0):
    operands = [pltpu.with_memory_space_constraint(x, pltpu.VMEM) for x in operands]
    results = pl.pallas_call(
        body,
        out_shape=[pltpu.VMEM(shape, F32) for shape in shapes],
        in_specs=[SPEC] * len(operands),
        out_specs=[SPEC] * len(shapes),
        scratch_shapes=[pltpu.VMEM(shape, F32) for shape in scratch],
        compiler_params=pltpu.CompilerParams(vmem_limit_bytes=24 << 20),
        cost_estimate=pl.CostEstimate(flops=flops, bytes_accessed=flops // 4, transcendentals=0),
    )(*operands)
    return list(results)


def head_body(s_ref, out, edge, sems):
    copies = []
    for half in range(2):
        for k in range(3):
            source = s_ref.at[k, pl.ds(9 * half, 6), 0]
            copies.append(pltpu.make_async_copy(source, out.at[k, half], sems.at[4 * half + k]))
        source = s_ref.at[0, pl.ds(9 * half, 6), 0]
        copies.append(pltpu.make_async_copy(source, edge.at[half], sems.at[4 * half + 3]))
    for copy in copies:
        copy.start()
    for copy in copies:
        copy.wait()


def head(dims, spatial):
    shape = (2, 6, dims.cols, dims.width)
    return pl.pallas_call(
        head_body,
        out_shape=[pltpu.VMEM((3, *shape), F32), pltpu.VMEM(shape, F32)],
        in_specs=[pl.BlockSpec(memory_space=pl.ANY)],
        out_specs=[SPEC] * 2,
        scratch_shapes=[pltpu.SemaphoreType.DMA((8,))],
        compiler_params=pltpu.CompilerParams(vmem_limit_bytes=4 << 20),
    )(spatial)


def third_row(ref, *index):
    out = []
    for j in range(3):
        m, n = (j + 1) % 3, (j + 2) % 3
        a, b = ref[(*index, 0, m)], ref[(*index, 1, m)]
        c, d = ref[(*index, 0, 3 + n)], ref[(*index, 1, 3 + n)]
        e, f = ref[(*index, 0, n)], ref[(*index, 1, n)]
        g, h = ref[(*index, 0, 3 + m)], ref[(*index, 1, 3 + m)]
        real = (a * c - b * d) - (e * g - f * h)
        imag = (a * d + b * c) - (e * h + f * g)
        out.append((real, -imag))
    return out


def gather(dims, source, even, odd, slot):
    for block in range(dims.blocks):
        lanes = slice(block * LANES, (block + 1) * LANES)
        for pair in range(dims.pairs):
            start = block * dims.group + pair * dims.cols
            rows = slice(start, start + dims.cols)
            even[slot, rows, :] = source(2 * pair, lanes)
            odd[slot, rows, :] = source(2 * pair + 1, lanes)


def ahead_of(dims, even, slot, out, *index):
    for block in range(dims.blocks):
        start = block * dims.group
        out[(*index, slice(start, start + dims.group - dims.cols))] = even[
            slot, start + dims.cols : start + dims.group
        ]


def edge_body(dims, t_ref, s_ref, q_ref, now, odd_x, next_x, msg_own, msg_other, even, odd, back):
    parity = parity_of(dims)
    last = iota((dims.rows, LANES), 0) // dims.cols % dims.pairs == dims.pairs - 1
    for c in range(18):
        gather(dims, lambda t, lanes: t_ref[c, t, :, lanes], even, odd, c)
        moved = y_move(dims, odd[c], -1)
        for q in range(2):
            q_ref[q, c] = jnp.where(parity == q, even[c], moved)
    for c in range(18):
        gather(dims, lambda t, lanes: s_ref[0, c, t, :, lanes], even, odd, c)
        value = odd[c]
        moved = y_move(dims, value, -1)
        for q in range(2):
            now[q, c] = jnp.where(parity == q, even[c], moved)
        odd_x[c] = value
        ahead_of(dims, even, c, next_x, c)
        even[c] = jnp.where(parity == 1, value, y_move(dims, next_x[c], -1))
    for rows in chunks(dims.rows):
        inner = product(matrix(q_ref, rows, 1), matrix(now, rows, 1), left_dagger=True)
        full = product(matrix(even, rows), inner, left_dagger=True)
        bare = (last & (parity == 0))[rows]
        put(
            back,
            rows,
            [
                (jnp.where(bare, a, c), jnp.where(bare, b, d))
                for (a, b), (c, d) in zip(inner, full)
            ],
        )
    emit(dims, q_ref.at[1], back, msg_own, msg_other)


def pack_body(dims, s_ref, r_ref, now_x, odd_x, next_x, now, odd_ref, next_ref, rot, even, odd):
    parity = parity_of(dims)
    for c in range(18):
        for q in range(2):
            now[q, 0, c] = now_x[q, c]
        odd_ref[0, c] = odd_x[c]
        next_ref[0, c] = next_x[c]

    def spatial(c, _):
        for k in range(1, 3):
            gather(dims, lambda t, lanes: s_ref[k, c, t, :, lanes], even, odd, k)
            moved = y_move(dims, odd[k], -1)
            for q in range(2):
                now[q, k, c] = jnp.where(parity == q, even[k], moved)
            odd_ref[k, c] = odd[k]
            ahead_of(dims, even, k, next_ref, k, c)
        return 0

    lax.fori_loop(0, 18, spatial, 0, unroll=3)

    def turns(sweep, _):
        for g in range(3):
            for c in range(4):
                slot = g * 4 + c
                gather(dims, lambda t, lanes: r_ref[sweep, g, c, t, :, lanes], even, odd, slot)
                moved = y_move(dims, odd[slot], -1)
                for q in range(2):
                    rot[sweep, q, g, c] = jnp.where(parity == q, even[slot], moved)
        return 0

    lax.fori_loop(0, dims.sweeps, turns, 0)


def arrange(dims, body, raw, packed, shapes, scratch, flops):
    packed = [pltpu.with_memory_space_constraint(x, pltpu.VMEM) for x in packed]
    return pl.pallas_call(
        functools.partial(body, dims),
        out_shape=[pltpu.VMEM(s, F32) for s in shapes],
        in_specs=[SPEC] * (len(raw) + len(packed)),
        out_specs=[SPEC] * len(shapes),
        scratch_shapes=[pltpu.VMEM(s, F32) for s in scratch],
        compiler_params=pltpu.CompilerParams(vmem_limit_bytes=24 << 20),
        cost_estimate=pl.CostEstimate(flops=flops, bytes_accessed=flops, transcendentals=0),
    )(*raw, *packed)


def emit(dims, links, back, msg_own, msg_other):
    even = lax.axis_index("sa") % 2 == 0

    def fill(right, left):
        for c in range(18):
            rows = slice(c * dims.edge, (c + 1) * dims.edge)
            right[rows, :] = back[c, pl.ds(dims.cols - 1, dims.edge, stride=dims.cols), :]
            left[rows, :] = links[c, pl.ds(0, dims.edge, stride=dims.cols), :]

    pl.when(even)(lambda: fill(msg_own, msg_other))
    pl.when(jnp.logical_not(even))(lambda: fill(msg_other, msg_own))


def absorb(dims, got_own, got_other, ahead, behind):
    even = lax.axis_index("sa") % 2 == 0

    def fill(from_right, from_left):
        for c in range(18):
            rows = slice(c * dims.edge, (c + 1) * dims.edge)
            ahead[c, pl.ds(dims.cols - 1, dims.edge, stride=dims.cols), :] = from_right[rows, :]
            behind[c, pl.ds(0, dims.edge, stride=dims.cols), :] = from_left[rows, :]

    pl.when(even)(lambda: fill(got_own, got_other))
    pl.when(jnp.logical_not(even))(lambda: fill(got_other, got_own))


def backward(dims, links, now, later, out, parity, direction):
    for rows in chunks(dims.rows):
        inner = product(
            matrix(links, rows), matrix(now, rows, parity, direction), left_dagger=True
        )
        put(
            out,
            rows,
            product(matrix(later, rows, parity, direction), inner, left_dagger=True),
        )


def first_body(dims, q, now, odd, nxt, nf, later, back, even):
    parity = parity_of(dims)
    last = dims.pairs - 1
    for k in range(3):
        third = third_row(nf, k)
        for c in range(18):
            half, entry = c // 9, c % 9
            value = nf[k, half, entry] if entry < 6 else third[entry - 6][half]
            for block in range(dims.blocks):
                start = block * dims.group
                middle = start + last * dims.cols
                even[c, start:middle] = nxt[k, c, start:middle]
                even[c, middle : start + dims.group] = value[
                    :, block * LANES : (block + 1) * LANES
                ]
            moved = y_move(dims, even[c], -1)
            value = odd[k, c]
            for p in range(2):
                later[p, k, c] = jnp.where(parity == p, value, moved)
    backward(dims, q.at[1], now, later, back, 1, 0)


def mend(dims, edge, behind, field):
    parity = parity_of(dims)
    row = iota((dims.rows, LANES), 0)
    last = dims.pairs - 1
    bare = (row // dims.cols % dims.pairs == last) & (row % dims.cols == 0) & (parity == 1)
    third = third_row(edge)
    for c in range(18):
        half, entry = c // 9, c % 9
        value = edge[half, entry] if entry < 6 else third[entry - 6][half]
        for block in range(dims.blocks):
            start = block * dims.group + last * dims.cols
            field[c, start : start + 1] = value[
                dims.cols - 1 :, block * LANES : (block + 1) * LANES
            ]
        field[c] = y_move(dims, field[c], -1)
    for rows in chunks(dims.rows):
        came = matrix(behind, rows)
        full = product(matrix(field, rows), came, left_dagger=True)
        put(
            behind,
            rows,
            [
                (jnp.where(bare[rows], a, c), jnp.where(bare[rows], b, d))
                for (a, b), (c, d) in zip(full, came)
            ],
        )


def inner_body(dims, p, other, now, later, out, moved, back):
    for direction, move in ((1, functools.partial(y_move, dims)), (2, z_move)):
        for c in range(18):
            moved[c] = move(other[c], 1)
        backward(dims, other, now, later, back, 1 - p, direction)
        for c in range(18):
            shifted = move(back[c], -1)
            out[c] = shifted if direction == 1 else out[c] + shifted
        for rows in chunks(dims.rows):
            half = product(matrix(now, rows, p, direction), matrix(moved, rows))
            term = product(matrix(later, rows, p, direction), half, right_dagger=True)
            put(out, rows, added(matrix(out, rows), term))


def rotate(entries, upper, lower, turn):
    a0, a1, a2, a3 = turn
    out = list(entries)
    for col in range(3):
        ur, ui = entries[3 * upper + col]
        lr, li = entries[3 * lower + col]
        out[3 * upper + col] = (
            (a0 * ur - a3 * ui) + (a2 * lr - a1 * li),
            (a0 * ui + a3 * ur) + (a2 * li + a1 * lr),
        )
        out[3 * lower + col] = (
            (a0 * lr + a3 * li) - (a2 * ur + a1 * ui),
            (a0 * li - a3 * lr) + (a1 * ur - a2 * ui),
        )
    return out


def update(links, staple, turns):
    field = product(links, staple)
    for g, (i, j) in enumerate(PAIRS):
        w0 = 0.5 * (field[4 * i][0] + field[4 * j][0])
        w1 = 0.5 * (field[3 * i + j][1] + field[3 * j + i][1])
        w2 = 0.5 * (field[3 * i + j][0] - field[3 * j + i][0])
        w3 = 0.5 * (field[4 * i][1] - field[4 * j][1])
        v = w1 * w1 + w2 * w2 + w3 * w3
        square = w0 * w0
        inverse = 1.0 / jnp.maximum(square + v, 0.5)
        r0 = (square - v) * inverse
        twice = (-2.0 * w0) * inverse
        r1, r2, r3 = twice * w1, twice * w2, twice * w3
        x0, x1, x2, x3 = turns[g]
        turn = (
            x0 * r0 - (x1 * r1 + x2 * r2 + x3 * r3),
            x0 * r1 + r0 * x1 - (x2 * r3 - x3 * r2),
            x0 * r2 + r0 * x2 - (x3 * r1 - x1 * r3),
            x0 * r3 + r0 * x3 - (x1 * r2 - x2 * r1),
        )
        links = rotate(links, i, j, turn)
        if g < 2:
            field = rotate(field, i, j, turn)
    return links


def outer_body(dims, p, sweep, last, *refs):
    own, other, now, later, rot, partial, back, got_own, got_other = refs[:9]
    begins = sweep == 0 and p == 0
    refs, edge = refs[9 + begins :], refs[9]
    new, ahead, behind = refs[0], refs[-2], refs[-1]
    for c in range(18):
        for col in range(dims.cols - 1):
            here = pl.ds(col, dims.edge, stride=dims.cols)
            there = pl.ds(col + 1, dims.edge, stride=dims.cols)
            ahead[c, here, :] = other[c, there, :]
            behind[c, there, :] = back[c, here, :]
    absorb(dims, got_own, got_other, ahead, behind)
    if begins:
        mend(dims, edge, behind, new)
    for rows in chunks(dims.rows):
        half = product(matrix(now, rows, p, 0), matrix(ahead, rows))
        term = product(matrix(later, rows, p, 0), half, right_dagger=True)
        staple = added(added(matrix(partial, rows), matrix(behind, rows)), term)
        turns = [[rot[sweep, p, g, c, rows] for c in range(4)] for g in range(3)]
        put(new, rows, update(matrix(own, rows), staple, turns))
    if not last:
        new_back, msg_own, msg_other = refs[1:4]
        backward(dims, new, now, later, new_back, p, 0)
        emit(dims, new, new_back, msg_own, msg_other)


def loop_body(dims, q0, q1, out, pair, parts):
    parity = parity_of(dims)
    for c in range(18):
        a, b = q0[c], q1[c]
        pair[0, c] = jnp.where(parity == 0, a, b)
        pair[1, c] = y_move(dims, jnp.where(parity == 0, b, a), 1)
    for rows in chunks(dims.rows):
        put(
            pair,
            rows,
            product(matrix(pair, rows, 0), matrix(pair, rows, 1)),
            2,
        )
    for c in range(18):
        for k in range(dims.pairs):
            for col in range(dims.cols):
                parts[k, c, pl.ds(col, dims.blocks, stride=dims.cols), :] = pair[
                    2, c, pl.ds(k * dims.cols + col, dims.blocks, stride=dims.group), :
                ]
    every = slice(0, dims.flat)
    total = matrix(parts, every, 0)
    for k in range(1, dims.pairs):
        total = product(total, matrix(parts, every, k))
    for c in range(9):
        for half in range(2):
            start = (9 * half + c) * dims.flat
            out[start : start + dims.flat, :] = total[c][half]


def merge_body(mine, got, out):
    near = lax.axis_index("ta") % 2
    out[near] = mine[...]
    out[1 - near] = got[...]


def chain_body(dims, distance, *refs):
    early = dims.sweeps - 1
    lines, crossed, pair, refs = refs[:early], refs[early : 2 * early], refs[2 * early], refs[2 * early + 1 :]
    begins, ends = distance == dims.far - 1, distance == 0
    if not begins:
        state, state_info, refs = refs[0], refs[1], refs[2:]
    out, out_info, sources, shifted, real_of, sum_of, gap_of, half, half_info = refs[:9]
    whole, whole_info = refs[9:] if ends else (out, out_info)
    place = lax.axis_index("ta")
    far, near = place // 2, place % 2
    rows = dims.flat
    shape = (rows, LANES)

    for s in range(early):
        sources[s, near] = lines[s][...]
        sources[s, 1 - near] = crossed[s][distance]

    def entry(s, h, c):
        here = slice(c * rows, (c + 1) * rows)
        return pair[h, here, :] if s == early else sources[s, h, here, :]

    def build(h, copy=None):
        for s in range(dims.sweeps):
            for c in range(18):
                shifted[s, c] = z_move(entry(s, h, c), DIST)
        total = jnp.zeros(shape, F32)
        for a in range(3):
            for e in range(3):
                at = 3 * a + e
                left = [
                    (
                        entry(s, h, at) * (1.0 / dims.sweeps),
                        entry(s, h, 9 + at)
                        * (1.0 / dims.sweeps),
                    )
                    for s in range(dims.sweeps)
                ]
                for c in range(3):
                    for d in range(3):
                        real = imag = None
                        for s in range(dims.sweeps):
                            lr, li = left[s]
                            pr, pi = shifted[s, 3 * c + d], shifted[s, 9 + 3 * c + d]
                            more_real, more_imag = lr * pr + li * pi, li * pr - lr * pi
                            real = more_real if real is None else real + more_real
                            imag = more_imag if imag is None else imag + more_imag
                        to = 9 * (3 * a + c) + 3 * e + d
                        real_of[to] = real
                        sum_of[to] = real + imag
                        gap_of[to] = imag - real
                        if copy is not None:
                            copy[to] = real
                            copy[81 + to] = imag
                        total = total + (real * real + imag * imag)
        return total

    def note(info, total, square, log):
        square_product = total / square / 162.0 + EPS
        info[0] = 1.0 / jnp.sqrt(square * square_product)
        info[1] = log + 0.5 * jnp.log(square) + 0.5 * jnp.log(square_product)

    def multiply(left, left_info, square, right, right_info):
        factor = left_info[0]

        def one_row(i, total):
            row = []
            for k in range(9):
                a, b = left[9 * i + k] * factor, left[81 + 9 * i + k] * factor
                row.append((a, b, a + b))
            for j in range(9):
                first = second = third = None
                for k in range(9):
                    a, b, ab = row[k]
                    to = 9 * k + j
                    x, y, z = real_of[to] * ab, sum_of[to] * b, gap_of[to] * a
                    first = x if first is None else first + x
                    second = y if second is None else second + y
                    third = z if third is None else third + z
                real, imag = first - second, first + third
                right[9 * i + j] = real
                right[81 + 9 * i + j] = imag
                total = total + (real * real + imag * imag)
            return total

        total = lax.fori_loop(0, 9, one_row, jnp.zeros(shape, F32))
        note(right_info, total, square, left_info[1])

    def start():
        total = build(0, half)
        note(half_info, total, total / 162.0 + EPS, jnp.zeros(shape, F32))

    def earlier():
        square = build(0) / 162.0 + EPS
        multiply(state, state_info, square, half, half_info)

    def later():
        square = build(1) / 162.0 + EPS
        multiply(half, half_info, square, whole, whole_info)

    def write(result, info):
        factor = info[0]
        for c in range(162):
            value = result[c] * factor
            for block in range(dims.blocks):
                here = slice(block * dims.cols, (block + 1) * dims.cols)
                out[c, :, block * LANES : (block + 1) * LANES] = value[here]
        for block in range(dims.blocks):
            here = slice(block * dims.cols, (block + 1) * dims.cols)
            out_info[:, block * LANES : (block + 1) * LANES] = info[1, here, :]

    if begins:
        pl.when(far >= distance)(start)
    else:
        pl.when(far == distance)(start)
        pl.when(far > distance)(earlier)
    if ends:

        @pl.when(near == 1)
        def _():
            later()
            write(whole, whole_info)

        pl.when(near == 0)(lambda: write(half, half_info))
    else:
        pl.when(far >= distance)(later)


def schedule(far, sweeps):
    windows = {w: [] for w in range(2, 2 * sweeps)}
    late = []
    for sweep in range(sweeps - 1):
        start = 2 * sweep + 2
        for d in range(far - 1, -1, -1):
            free = [w for w in range(start, 2 * sweeps) if len(windows[w]) < 2]
            if free:
                windows[free[0]].append((sweep, d))
                start = max(start, free[0] + (d == 1))
            else:
                late.append((sweep, d))
                start = 2 * sweeps
    return windows, late


def join_body(*refs):
    for i, ref in enumerate(refs[:-1]):
        refs[-1][i] = ref[...]


class Transport:
    def __init__(self, dims):
        self.dims, self.loops, self.lines, self.crossed = dims, [], [], []
        self.windows, self.late = schedule(dims.far, dims.sweeps)

    def send(self, value, d):
        n = self.dims.ta
        return lax.ppermute(value, "ta", [(i, (i + 2 * d) % n) for i in range(n)])

    def swap(self, value):
        return lax.ppermute(value, "ta", [(i, i ^ 1) for i in range(self.dims.ta)])

    def move(self, sweep, d):
        if sweep == len(self.lines):
            self.lines.append({0: self.loops[sweep]})
        line = self.lines[sweep]
        if d:
            line[d] = self.send(line[0], d)
            return
        (blocks,) = call(
            join_body,
            [line[i] for i in range(self.dims.far)],
            [(self.dims.far, self.dims.loop_rows, LANES)],
        )
        self.crossed.append(self.swap(blocks))

    def window(self, w):
        for sweep, d in self.windows.get(w, ()):
            self.move(sweep, d)

    def finish(self):
        last = self.dims.sweeps - 1
        got = self.swap(self.loops[last])
        for sweep, d in self.late:
            self.move(sweep, d)
        (pair,) = call(
            merge_body,
            [self.loops[last], got],
            [(2, self.dims.loop_rows, LANES)],
        )
        self.pairs = {0: pair}
        for d in range(self.dims.far - 1, 0, -1):
            self.pairs[d] = self.send(pair, d)

    def operands(self, d):
        return [line[d] for line in self.lines] + self.crossed + [self.pairs[d]]


def per_device(ta, sa, temporal, spatial, rotations):
    dims = Dims(temporal, rotations, ta, sa)
    shape = (dims.rows, LANES)
    message = (18 * dims.edge, LANES)
    nf, edge = head(dims, spatial)
    nf = lax.ppermute(nf, "ta", [((i + 1) % ta, i) for i in range(ta)])
    field = (18, *shape)
    q, now_x, odd_x, next_x, msg_own, msg_other = arrange(
        dims,
        edge_body,
        [temporal, spatial],
        [],
        [(2, *field), (2, *field), field, field, message, message],
        [field] * 3,
        2000000,
    )
    now, odd, nxt, rot = arrange(
        dims,
        pack_body,
        [spatial, rotations],
        [now_x, odd_x, next_x],
        [(2, 3, *field), (3, *field), (3, *field), (dims.sweeps, 2, 3, 4, *shape)],
        [(12, *shape)] * 2,
        4000000,
    )
    corners = [
        ((i + 1) % ta * sa + j, i * sa + (j + 1) % sa) for i in range(ta) for j in range(sa)
    ]
    edge = lax.ppermute(edge, ("ta", "sa"), corners)
    later, back = call(
        functools.partial(first_body, dims),
        [q, now, odd, nxt, nf],
        [(2, 3, *field), field],
        [field],
        flops=2000000,
    )
    fields = [q[0], q[1]]
    own_pairs = [(i, i ^ 1) for i in range(sa)]
    other_pairs = [(i, (i + 1) % sa if i % 2 else (i - 1) % sa) for i in range(sa)]
    transport = Transport(dims)
    for sweep in range(dims.sweeps):
        for p in range(2):
            last = sweep == dims.sweeps - 1 and p == 1
            w = 2 * sweep + p
            got_other = lax.ppermute(msg_other, "sa", other_pairs)
            got_own = lax.ppermute(msg_own, "sa", own_pairs)
            (partial,) = call(
                functools.partial(inner_body, dims, p),
                [fields[1 - p], now, later],
                [(18, *shape)],
                [(18, *shape), (18, *shape)],
                flops=3000000,
            )
            transport.window(w)
            outs = [(18, *shape)] + ([] if last else [(18, *shape), message, message])
            result = call(
                functools.partial(outer_body, dims, p, sweep, last),
                [fields[p], fields[1 - p], now, later, rot, partial, back, got_own, got_other]
                + ([edge] if w == 0 else []),
                outs,
                [(18, *shape), (18, *shape)],
                flops=3000000,
            )
            fields[p] = result[0]
            if not last:
                back, msg_own, msg_other = result[1:]
        (loop,) = call(
            functools.partial(loop_body, dims),
            fields,
            [(dims.loop_rows, LANES)],
            [(3, 18, *shape), (dims.pairs, 18, dims.flat, LANES)],
            flops=1000000,
        )
        transport.loops.append(loop)
    transport.finish()
    log = (dims.flat, LANES)
    field, info, third = (162, *log), (2, *log), (81, *log)
    scratch = [
        (dims.sweeps - 1, 2, dims.loop_rows, LANES),
        (dims.sweeps, 18, *log),
        third,
        third,
        third,
        field,
        info,
    ]
    state = []
    for d in range(dims.far - 1, 0, -1):
        state = call(
            functools.partial(chain_body, dims, d),
            transport.operands(d) + state,
            [field, info],
            scratch,
            flops=10000000,
        )
    operands = [
        pltpu.with_memory_space_constraint(x, pltpu.VMEM)
        for x in transport.operands(0) + state
    ]
    transfer, log_scale = pl.pallas_call(
        functools.partial(chain_body, dims, 0),
        out_shape=[
            jax.ShapeDtypeStruct((162, dims.cols, dims.width), F32),
            jax.ShapeDtypeStruct((dims.cols, dims.width), F32),
        ],
        in_specs=[SPEC] * len(operands),
        out_specs=[SPEC] * 2,
        scratch_shapes=[pltpu.VMEM(x, F32) for x in scratch + [field, info]],
        compiler_params=pltpu.CompilerParams(vmem_limit_bytes=16 << 20),
    )(*operands)
    return (
        transfer.reshape(2, 9, 9, 1, dims.cols, dims.width),
        log_scale[None],
    )


def solution(mesh):
    in_specs = (
        P(None, "ta", "sa", None),
        P(None, None, "ta", "sa", None),
        P(None, None, None, "ta", "sa", None),
    )
    out_specs = (P(None, None, None, "ta", "sa", None), P("ta", "sa", None))
    body = functools.partial(per_device, mesh.shape["ta"], mesh.shape["sa"])
    return jax.shard_map(
        body, mesh=mesh, in_specs=in_specs, out_specs=out_specs, check_vma=False
    )
```
